32 devices in a mesh: sensor: 8 (over y, x, core), tm: 4 (over z).
Axes of the slice: x: 2, y: 2, z: 4, core: 2. Of those that a mesh axis runs over, the one named last changes fastest.
Arguments:
- series: bfloat16 [12, 1024, 128], P('tm', 'sensor'), may hold values from -40 to 40
- conv_weight: bfloat16 [3, 128, 256], replicated, may hold values from -0.3125 to 0.3125
- qk_weight: bfloat16 [2, 128, 128], replicated, may hold values from -1 to 1
- value_weight: bfloat16 [128, 128], replicated, may hold values from -0.5 to 0.5
- out_weight: bfloat16 [128, 128], replicated, may hold values from -0.5 to 0.5
- norm_gain: float32 [128], replicated, may hold values from 0.25 to 1.75
Outputs:
- layer_out: bfloat16 [12, 1024, 128], P('tm', 'sensor')
The draws below stay inside these ranges and needn't reach their ends.
All inputs are finite; a program needn't handle non-finite values.
Results may differ from the reference program's by a relative error of at most 0.012.
The reference program's roundings to bfloat16 on the way (of `hidden` and `attended`) count: a program that leaves them out, or rounds other values in their place, can miss the bound.
Values may be sent and summed in bfloat16 or wider, within the bound.
A program may use at most 64 MiB of HBM per device.

```python
import math
import jax
import jax.numpy as jnp
from jax import lax

D = 128
HEADS = 8
KERNEL = 3
SENSORS = 1024
STEPS = 12


def draw_series(key, part):
    groups = 8
    pieces = jax.random.split(jax.random.fold_in(key, 5), 4)
    patterns = 1.2 * jax.random.truncated_normal(pieces[0], -3.0, 3.0, (groups, D), jnp.float32)
    members = jax.random.randint(pieces[1], (SENSORS,), 0, groups)
    chosen = patterns[members]
    noise_scale = jax.random.uniform(pieces[2], (1, SENSORS, 1), jnp.float32, 0.25, 1.5)
    noise = 0.7 * jax.random.truncated_normal(pieces[3], -4.0, 4.0, (STEPS, SENSORS, D), jnp.float32)
    return (chosen[None, :, :] + noise_scale * noise).astype(jnp.bfloat16)


def draw_qk_weight(key, part):
    pieces = jax.random.split(jax.random.fold_in(key, 11), 2)
    base = jax.random.truncated_normal(pieces[0], -4.0, 4.0, (D, D), jnp.float32) * D ** (-0.5)
    noise = jax.random.truncated_normal(pieces[1], -4.0, 4.0, (D, D), jnp.float32) * D ** (-0.5)
    return jnp.stack([base, 0.8 * base + 0.6 * noise]).astype(jnp.bfloat16)


def centred(rng, extent, deviation, most, held_as=jnp.bfloat16):
    entries = jax.random.normal(rng, extent, jnp.float32) * deviation
    return jnp.minimum(jnp.maximum(entries, -most), most).astype(held_as)


def setup_inputs(seed: int = 0) -> dict:
    arg_keys = jax.random.split(jax.random.key(seed), 7)
    series = draw_series(jax.random.fold_in(arg_keys[6], 71), 0)
    conv_weight = centred(arg_keys[1], (KERNEL, D, 2 * D), (KERNEL * D) ** -0.5, 0.3125)
    qk_weight = draw_qk_weight(jax.random.fold_in(arg_keys[6], 71), 0)
    value_weight = centred(arg_keys[3], (D, D), D ** -0.5, 0.5)
    out_weight = centred(arg_keys[4], (D, D), D ** -0.5, 0.5)
    norm_gain = jnp.clip(1.0 + 0.15 * jax.random.normal(arg_keys[5], (D,), jnp.float32), 0.25, 1.75)
    return dict(series=series, conv_weight=conv_weight, qk_weight=qk_weight, value_weight=value_weight, out_weight=out_weight, norm_gain=norm_gain)


def reference(series, conv_weight, qk_weight, value_weight, out_weight, norm_gain):
    head_dim = D // HEADS
    scale = 1.0 / math.sqrt(head_dim)
    zeros = jnp.zeros((KERNEL - 1, SENSORS, D), series.dtype)
    padded = jnp.concatenate([zeros, series], axis=0)
    conv = jnp.zeros((STEPS * SENSORS, 2 * D), jnp.float32)
    for tap in range(KERNEL):
        window = padded[KERNEL - 1 - tap:KERNEL - 1 - tap + STEPS].reshape(STEPS * SENSORS, D)
        conv = conv + jnp.dot(window, conv_weight[tap], preferred_element_type=jnp.float32)
    flat = series.reshape(STEPS * SENSORS, D).astype(jnp.float32)
    hidden = (flat + conv[:, :D] * jax.nn.sigmoid(conv[:, D:])).astype(jnp.bfloat16)
    query = jnp.dot(hidden, qk_weight[0], preferred_element_type=jnp.float32).astype(jnp.bfloat16)
    keys = jnp.dot(hidden, qk_weight[1], preferred_element_type=jnp.float32).astype(jnp.bfloat16)
    values = jnp.dot(hidden, value_weight, preferred_element_type=jnp.float32).astype(jnp.bfloat16)
    query = query.reshape(STEPS, SENSORS, HEADS, head_dim)
    keys = keys.reshape(STEPS, SENSORS, HEADS, head_dim)
    values = values.reshape(STEPS, SENSORS, HEADS, head_dim)
    block = math.gcd(SENSORS, 512)
    nblocks = SENSORS // block

    def one_step(operands):
        q_step, k_step, v_step = operands
        k_wide = k_step.astype(jnp.float32)
        v_wide = v_step.astype(jnp.float32)

        def one_block(q_block):
            scores = jnp.einsum('bhd,khd->hbk', q_block.astype(jnp.float32), k_wide) * scale
            rowmax = lax.optimization_barrier(jnp.max(scores, axis=-1))
            probs = jnp.exp(scores - rowmax[..., None])
            total = lax.optimization_barrier(jnp.sum(probs, axis=-1))
            weighted = probs.astype(jnp.bfloat16).astype(jnp.float32)
            summed = jnp.einsum('hbk,khd->bhd', weighted, v_wide)
            return summed / jnp.transpose(total)[..., None]
        blocks = lax.map(one_block, q_step.reshape(nblocks, block, HEADS, head_dim))
        return blocks.reshape(SENSORS, HEADS, head_dim)
    attended = lax.map(one_step, (query, keys, values))
    attended = attended.reshape(STEPS * SENSORS, D).astype(jnp.bfloat16)
    mixed = jnp.dot(attended, out_weight, preferred_element_type=jnp.float32) + hidden.astype(jnp.float32)
    mean = lax.optimization_barrier(jnp.mean(mixed, axis=-1, keepdims=True))
    var = lax.optimization_barrier(jnp.mean((mixed - mean) ** 2, axis=-1, keepdims=True))
    normed = (mixed - mean) / jnp.sqrt(var + 1e-05) * norm_gain
    return normed.reshape(STEPS, SENSORS, D).astype(jnp.bfloat16)
```

```python
import functools
import math

import jax
import jax.numpy as jnp
from jax import lax
from jax.experimental import pallas as pl
from jax.experimental.pallas import tpu as pltpu
from jax.sharding import PartitionSpec as P

HEADS = 8
MESH = pl.DeviceIdType.MESH


def kernel(
    n,
    blocks,
    series_hbm,
    conv_hbm,
    qk_hbm,
    value_hbm,
    out_w_hbm,
    gain_hbm,
    out_ref,
    ext,
    conv_w,
    qk_w,
    kv_w,
    out_w,
    gain,
    gathered,
    key_ref,
    val_ref,
    load_sem,
    halo_send,
    halo_recv,
    peer_send,
    peer_recv,
    fwd_send,
    fwd_recv,
):
    steps, sens, width = out_ref.shape
    taps = conv_w.shape[0]
    lead = taps - 1
    pairs = n // 2
    head_dim = width // HEADS
    factor = math.log2(math.e) / math.sqrt(head_dim)
    me = lax.axis_index("sensor")
    here = lax.axis_index("tm")
    pair, core = me // 2, me % 2
    partner = pair * 2 + 1 - core

    loads = [
        pltpu.make_async_copy(series_hbm, ext.at[pl.ds(lead, steps)], load_sem.at[0]),
        pltpu.make_async_copy(conv_hbm, conv_w, load_sem.at[1]),
        pltpu.make_async_copy(qk_hbm, qk_w, load_sem.at[2]),
        pltpu.make_async_copy(value_hbm, kv_w, load_sem.at[3]),
        pltpu.make_async_copy(out_w_hbm, out_w, load_sem.at[4]),
        pltpu.make_async_copy(gain_hbm, gain, load_sem.at[5]),
    ]
    for load in loads:
        load.start()

    def peer(j):
        return ((pair + j) % pairs) * 2 + core

    barrier = pltpu.get_barrier_semaphore()
    pl.semaphore_signal(barrier, inc=1, device_id={"sensor": partner}, device_id_type=MESH)
    for j in range(1, pairs):
        pl.semaphore_signal(barrier, inc=1, device_id={"sensor": peer(j)}, device_id_type=MESH)

    @pl.when(here > 0)
    def _():
        pl.semaphore_signal(barrier, inc=1, device_id={"tm": here - 1}, device_id_type=MESH)

    @pl.when(here < blocks - 1)
    def _():
        pl.semaphore_signal(barrier, inc=1, device_id={"tm": here + 1}, device_id_type=MESH)

    @pl.when(here == 0)
    def _():
        ext[pl.ds(0, lead)] = jnp.zeros((lead, sens, width), ext.dtype)

    val_ref[:, width:] = jnp.ones((n * sens, width), val_ref.dtype)

    loads[0].wait()
    behind = (here + blocks - 1) // blocks
    ahead = (2 * blocks - 2 - here) // blocks
    pl.semaphore_wait(barrier, pairs + behind + ahead)

    def halo(i):
        return pltpu.make_async_remote_copy(
            src_ref=ext.at[steps + i],
            dst_ref=ext.at[i],
            send_sem=halo_send.at[i],
            recv_sem=halo_recv.at[i],
            device_id={"tm": here + 1},
            device_id_type=MESH,
        )

    @pl.when(here < blocks - 1)
    def _():
        for i in reversed(range(lead)):
            halo(i).start()

    def send(t, j):
        return pltpu.make_async_remote_copy(
            src_ref=gathered.at[t, 0, 0],
            dst_ref=gathered.at[t, 0, j],
            send_sem=peer_send.at[t, j],
            recv_sem=peer_recv.at[t, j],
            device_id={"sensor": peer(j)},
            device_id_type=MESH,
        )

    def forward(t, j):
        return pltpu.make_async_remote_copy(
            src_ref=gathered.at[t, 0, j],
            dst_ref=gathered.at[t, 1, j],
            send_sem=fwd_send.at[t, j],
            recv_sem=fwd_recv.at[t, j],
            device_id={"sensor": partner},
            device_id_type=MESH,
        )

    loads[1].wait()
    for t in reversed(range(steps)):
        if t < lead:

            @pl.when(here > 0)
            def _():
                halo(t).wait_recv()

        conv = jnp.dot(ext[lead + t], conv_w[0], preferred_element_type=jnp.float32)
        for tap in range(1, taps):
            conv = conv + jnp.dot(
                ext[lead + t - tap], conv_w[tap], preferred_element_type=jnp.float32
            )
        own = ext[lead + t].astype(jnp.float32)
        own = own + conv[:, :width] * jax.nn.sigmoid(conv[:, width:])
        gathered[t, 0, 0] = own.astype(gathered.dtype)
        for j in range(1, pairs):
            send(t, j).start()
        forward(t, 0).start()

    for load in loads[2:]:
        load.wait()

    def pass_on(t):
        for j in range(1, pairs):
            send(t, j).wait_recv()
            forward(t, j).start()

    lanes = lax.broadcasted_iota(jnp.int32, (sens, width), 1)
    chunk = min(n * sens, 1024)
    chunks = n * sens // chunk

    def head_parts(query, h):
        mine = (lanes >= h * head_dim) & (lanes < (h + 1) * head_dim)
        masked = jnp.where(mine, query, jnp.zeros_like(query)).astype(jnp.bfloat16)

        def scores_of(c):
            start = c * chunk if isinstance(c, int) else pl.multiple_of(c * chunk, chunk)
            keys = key_ref[pl.ds(start, chunk)]
            scores = lax.dot_general(
                masked, keys, (((1,), (1,)), ((), ())), preferred_element_type=jnp.float32
            )
            return scores, val_ref[pl.ds(start, chunk)]

        if chunks == 1:
            scores, values = scores_of(0)
            top = jnp.max(scores, axis=-1, keepdims=True)
            probs = jnp.exp2((scores - top) * factor).astype(jnp.bfloat16)
            summed = jnp.dot(probs, values, preferred_element_type=jnp.float32)
            return mine, summed

        def one(c, carry):
            maxima, summed = carry
            scores, values = scores_of(c)
            top = jnp.maximum(maxima, jnp.max(scores, axis=-1, keepdims=True))
            probs = jnp.exp2((scores - top) * factor).astype(jnp.bfloat16)
            added = jnp.dot(probs, values, preferred_element_type=jnp.float32)
            return top, summed * jnp.exp2((maxima - top) * factor) + added

        state = (
            jnp.full((sens, 1), -3e38, jnp.float32),
            jnp.zeros((sens, 2 * width), jnp.float32),
        )
        return mine, lax.fori_loop(0, chunks, one, state)[1]

    pass_on(steps - 1)
    for t in reversed(range(steps)):
        for j in range(pairs):
            forward(t, j).wait_recv()
        rows = gathered[t].reshape(n * sens, width)
        key_ref[...] = jnp.dot(rows, qk_w[1], preferred_element_type=jnp.float32).astype(
            jnp.bfloat16
        )
        val_ref[:, :width] = jnp.dot(
            rows, kv_w[...], preferred_element_type=jnp.float32
        ).astype(jnp.bfloat16)
        hidden = gathered[t, 0, 0]
        query = jnp.dot(hidden, qk_w[0], preferred_element_type=jnp.float32)
        query = query.astype(jnp.bfloat16).astype(jnp.float32)
        top_part = jnp.zeros((sens, width), jnp.float32)
        total = jnp.ones((sens, width), jnp.float32)
        for h in range(HEADS):
            if h == HEADS // 2 and t > 0:
                pass_on(t - 1)
            mine, summed = head_parts(query, h)
            top_part = jnp.where(mine, summed[:, :width], top_part)
            total = jnp.where(mine, summed[:, width:], total)
        attended = (top_part / total).astype(jnp.bfloat16)
        mixed = jnp.dot(attended, out_w[...], preferred_element_type=jnp.float32)
        mixed = mixed + hidden.astype(jnp.float32)
        mean = jnp.mean(mixed, axis=-1, keepdims=True)
        centred = mixed - mean
        var = jnp.mean(centred * centred, axis=-1, keepdims=True)
        normed = centred / jnp.sqrt(var + 1e-05) * gain[...]
        out_ref[t] = normed.astype(out_ref.dtype)

    for t in range(steps):
        for j in range(1, pairs):
            send(t, j).wait_send()
        for j in range(pairs):
            forward(t, j).wait_send()

    @pl.when(here < blocks - 1)
    def _():
        for i in range(lead):
            halo(i).wait_send()


def solution(mesh):
    n, blocks = mesh.shape["sensor"], mesh.shape["tm"]

    def local(series, conv_weight, qk_weight, value_weight, out_weight, norm_gain):
        steps, sens, width = series.shape
        taps = conv_weight.shape[0]
        pairs = n // 2
        bf16 = jnp.bfloat16
        return pl.pallas_call(
            functools.partial(kernel, n, blocks),
            out_shape=jax.ShapeDtypeStruct(series.shape, bf16),
            in_specs=[pl.BlockSpec(memory_space=pl.ANY)] * 6,
            out_specs=pl.BlockSpec(memory_space=pltpu.VMEM),
            scratch_shapes=[
                pltpu.VMEM((taps - 1 + steps, sens, width), bf16),
                pltpu.VMEM(conv_weight.shape, bf16),
                pltpu.VMEM(qk_weight.shape, bf16),
                pltpu.VMEM(value_weight.shape, bf16),
                pltpu.VMEM(out_weight.shape, bf16),
                pltpu.VMEM((1, width), jnp.float32),
                pltpu.VMEM((steps, 2, pairs, sens, width), bf16),
                pltpu.VMEM((n * sens, width), bf16),
                pltpu.VMEM((n * sens, 2 * width), bf16),
                pltpu.SemaphoreType.DMA((6,)),
                pltpu.SemaphoreType.DMA((taps - 1,)),
                pltpu.SemaphoreType.DMA((taps - 1,)),
                pltpu.SemaphoreType.DMA((steps, pairs)),
                pltpu.SemaphoreType.DMA((steps, pairs)),
                pltpu.SemaphoreType.DMA((steps, pairs)),
                pltpu.SemaphoreType.DMA((steps, pairs)),
            ],
            compiler_params=pltpu.CompilerParams(collective_id=0, has_side_effects=True),
        )(
            series,
            conv_weight,
            qk_weight,
            value_weight,
            out_weight,
            norm_gain.reshape(1, width),
        )

    in_specs = (P("tm", "sensor", None), P(), P(), P(), P(), P())
    out_specs = P("tm", "sensor", None)
    return jax.shard_map(local, mesh=mesh, in_specs=in_specs, out_specs=out_specs, check_vma=False)
```

```python
import functools
import math

import jax
import jax.numpy as jnp
from jax import lax
from jax.experimental import pallas as pl
from jax.experimental.pallas import tpu as pltpu
from jax.sharding import PartitionSpec as P

HEADS = 8
MESH = pl.DeviceIdType.MESH


def kernel(
    n,
    blocks,
    series_hbm,
    conv_hbm,
    qk_hbm,
    value_hbm,
    out_w_hbm,
    gain_hbm,
    out_ref,
    ext,
    conv_w,
    q_w,
    kv_w,
    out_w,
    gain,
    gathered,
    query_ref,
    key_ref,
    val_ref,
    load_sem,
    halo_send,
    halo_recv,
    peer_send,
    peer_recv,
    fwd_send,
    fwd_recv,
):
    steps, sens, width = out_ref.shape
    taps = conv_w.shape[0]
    lead = taps - 1
    pairs = n // 2
    head_dim = width // HEADS
    factor = math.log2(math.e) / math.sqrt(head_dim)
    me = lax.axis_index("sensor")
    here = lax.axis_index("tm")
    pair, core = me // 2, me % 2
    partner = pair * 2 + 1 - core

    loads = [
        pltpu.make_async_copy(series_hbm, ext.at[pl.ds(lead, steps)], load_sem.at[0]),
        pltpu.make_async_copy(conv_hbm, conv_w, load_sem.at[1]),
        pltpu.make_async_copy(qk_hbm.at[0], q_w, load_sem.at[2]),
        pltpu.make_async_copy(qk_hbm.at[1], kv_w.at[:, pl.ds(0, width)], load_sem.at[3]),
        pltpu.make_async_copy(value_hbm, kv_w.at[:, pl.ds(width, width)], load_sem.at[4]),
        pltpu.make_async_copy(out_w_hbm, out_w, load_sem.at[5]),
        pltpu.make_async_copy(gain_hbm, gain, load_sem.at[6]),
    ]
    for load in loads:
        load.start()

    def peer(j):
        return ((pair + j) % pairs) * 2 + core

    barrier = pltpu.get_barrier_semaphore()
    pl.semaphore_signal(barrier, inc=1, device_id={"sensor": partner}, device_id_type=MESH)
    for j in range(1, pairs):
        pl.semaphore_signal(barrier, inc=1, device_id={"sensor": peer(j)}, device_id_type=MESH)

    @pl.when(here > 0)
    def _():
        pl.semaphore_signal(barrier, inc=1, device_id={"tm": here - 1}, device_id_type=MESH)

    @pl.when(here < blocks - 1)
    def _():
        pl.semaphore_signal(barrier, inc=1, device_id={"tm": here + 1}, device_id_type=MESH)

    @pl.when(here == 0)
    def _():
        ext[pl.ds(0, lead)] = jnp.zeros((lead, sens, width), ext.dtype)

    val_ref[:, :, width:] = jnp.ones((steps, n * sens, width), val_ref.dtype)

    loads[0].wait()
    behind = (here + blocks - 1) // blocks
    ahead = (2 * blocks - 2 - here) // blocks
    pl.semaphore_wait(barrier, pairs + behind + ahead)

    def halo(i):
        return pltpu.make_async_remote_copy(
            src_ref=ext.at[steps + i],
            dst_ref=ext.at[i],
            send_sem=halo_send.at[i],
            recv_sem=halo_recv.at[i],
            device_id={"tm": here + 1},
            device_id_type=MESH,
        )

    @pl.when(here < blocks - 1)
    def _():
        for i in reversed(range(lead)):
            halo(i).start()

    def send(t, j):
        return pltpu.make_async_remote_copy(
            src_ref=gathered.at[t, 0, 0],
            dst_ref=gathered.at[t, j, 0],
            send_sem=peer_send.at[t, j],
            recv_sem=peer_recv.at[t, j],
            device_id={"sensor": peer(j)},
            device_id_type=MESH,
        )

    def forward(t, j):
        return pltpu.make_async_remote_copy(
            src_ref=gathered.at[t, j, 0],
            dst_ref=gathered.at[t, j, 1],
            send_sem=fwd_send.at[t, j],
            recv_sem=fwd_recv.at[t, j],
            device_id={"sensor": partner},
            device_id_type=MESH,
        )

    lanes = lax.broadcasted_iota(jnp.int32, (sens, width), 1)
    mine = [(lanes >= h * head_dim) & (lanes < (h + 1) * head_dim) for h in range(HEADS)]

    def prepare(t):
        if t < lead:

            @pl.when(here > 0)
            def _():
                halo(t).wait_recv()

        conv = jnp.dot(ext[lead + t], conv_w[0], preferred_element_type=jnp.float32)
        for tap in range(1, taps):
            conv = conv + jnp.dot(
                ext[lead + t - tap], conv_w[tap], preferred_element_type=jnp.float32
            )
        own = ext[lead + t].astype(jnp.float32)
        own = own + conv[:, :width] * jax.nn.sigmoid(conv[:, width:])
        gathered[t, 0, 0] = own.astype(gathered.dtype)
        for j in range(1, pairs):
            send(t, j).start()
        forward(t, 0).start()

    def queries(t):
        query = jnp.dot(gathered[t, 0, 0], q_w[...], preferred_element_type=jnp.float32)
        for h in range(HEADS):
            query_ref[t, h] = jnp.where(mine[h], query, 0.0).astype(jnp.bfloat16)

    def pass_on(t):
        for j in range(1, pairs):
            send(t, j).wait_recv()
            forward(t, j).start()

    def absorb(t, rows, start):
        count = rows.shape[0]
        place = pl.ds(start, count)
        both = jnp.dot(rows, kv_w[...], preferred_element_type=jnp.float32)
        key_ref[t, place] = both[:, :width].astype(jnp.bfloat16)
        val_ref[t, place, :width] = both[:, width:].astype(jnp.bfloat16)
        maxima = weighted = total = jnp.zeros((sens, width), jnp.float32)
        for h in range(HEADS):
            scores = lax.dot_general(
                query_ref[t, h],
                key_ref[t, place],
                (((1,), (1,)), ((), ())),
                preferred_element_type=jnp.float32,
            )
            top = jnp.max(scores, axis=-1, keepdims=True)
            probs = jnp.exp2((scores - top) * factor).astype(jnp.bfloat16)
            summed = jnp.dot(probs, val_ref[t, place], preferred_element_type=jnp.float32)
            maxima = jnp.where(mine[h], top, maxima)
            weighted = jnp.where(mine[h], summed[:, :width], weighted)
            total = jnp.where(mine[h], summed[:, width:], total)
        return maxima, weighted, total

    def merge(states):
        maxima = functools.reduce(jnp.maximum, [state[0] for state in states])
        weighted = total = 0.0
        for state in states:
            share = jnp.exp2((state[0] - maxima) * factor)
            weighted = weighted + state[1] * share
            total = total + state[2] * share
        return maxima, weighted, total

    states = [[] for _ in range(steps)]

    def near(t):
        forward(t, 0).wait_recv()
        states[t].append(absorb(t, gathered[t, 0].reshape(2 * sens, width), 0))

    def far(t, side):
        if side:
            for j in range(1, pairs):
                forward(t, j).wait_recv()
        if pairs <= 4:
            rows = gathered[t, pl.ds(1, pairs - 1), side].reshape((pairs - 1) * sens, width)
            start = (2 + side * (pairs - 1)) * sens
            states[t].append(absorb(t, rows, start))
            return

        def one(j, state):
            return merge([state, absorb(t, gathered[t, j, side], 0)])

        states[t] = [lax.fori_loop(1, pairs, one, merge(states[t]))]

    def finish(t):
        _, weighted, total = merge(states[t])
        attended = (weighted / total).astype(jnp.bfloat16)
        mixed = jnp.dot(attended, out_w[...], preferred_element_type=jnp.float32)
        mixed = mixed + gathered[t, 0, 0].astype(jnp.float32)
        mean = jnp.mean(mixed, axis=-1, keepdims=True)
        centred = mixed - mean
        var = jnp.mean(centred * centred, axis=-1, keepdims=True)
        normed = centred / jnp.sqrt(var + 1e-05) * gain[...]
        out_ref[t] = normed.astype(out_ref.dtype)

    last = steps - 1
    loads[1].wait()
    prepare(last)
    for load in loads[2:]:
        load.wait()
    queries(last)
    near(last)
    for t in reversed(range(last)):
        prepare(t)
        queries(t)
    if last > 0:
        near(last - 1)
    pass_on(last)
    for t in reversed(range(last - 1)):
        near(t)
    for t in reversed(range(steps)):
        far(t, 0)
        far(t, 1)
        if t > 0:
            pass_on(t - 1)
        finish(t)

    for t in range(steps):
        for j in range(1, pairs):
            send(t, j).wait_send()
        for j in range(pairs):
            forward(t, j).wait_send()

    @pl.when(here < blocks - 1)
    def _():
        for i in range(lead):
            halo(i).wait_send()


def solution(mesh):
    n, blocks = mesh.shape["sensor"], mesh.shape["tm"]

    def local(series, conv_weight, qk_weight, value_weight, out_weight, norm_gain):
        steps, sens, width = series.shape
        taps = conv_weight.shape[0]
        pairs = n // 2
        bf16 = jnp.bfloat16
        return pl.pallas_call(
            functools.partial(kernel, n, blocks),
            out_shape=jax.ShapeDtypeStruct(series.shape, bf16),
            in_specs=[pl.BlockSpec(memory_space=pl.ANY)] * 6,
            out_specs=pl.BlockSpec(memory_space=pltpu.VMEM),
            scratch_shapes=[
                pltpu.VMEM((taps - 1 + steps, sens, width), bf16),
                pltpu.VMEM(conv_weight.shape, bf16),
                pltpu.VMEM((width, width), bf16),
                pltpu.VMEM((width, 2 * width), bf16),
                pltpu.VMEM(out_weight.shape, bf16),
                pltpu.VMEM((1, width), jnp.float32),
                pltpu.VMEM((steps, pairs, 2, sens, width), bf16),
                pltpu.VMEM((steps, HEADS, sens, width), bf16),
                pltpu.VMEM((steps, n * sens, width), bf16),
                pltpu.VMEM((steps, n * sens, 2 * width), bf16),
                pltpu.SemaphoreType.DMA((7,)),
                pltpu.SemaphoreType.DMA((taps - 1,)),
                pltpu.SemaphoreType.DMA((taps - 1,)),
                pltpu.SemaphoreType.DMA((steps, pairs)),
                pltpu.SemaphoreType.DMA((steps, pairs)),
                pltpu.SemaphoreType.DMA((steps, pairs)),
                pltpu.SemaphoreType.DMA((steps, pairs)),
            ],
            compiler_params=pltpu.CompilerParams(collective_id=0, has_side_effects=True),
        )(
            series,
            conv_weight,
            qk_weight,
            value_weight,
            out_weight,
            norm_gain.reshape(1, width),
        )

    in_specs = (P("tm", "sensor", None), P(), P(), P(), P(), P())
    out_specs = P("tm", "sensor", None)
    return jax.shard_map(local, mesh=mesh, in_specs=in_specs, out_specs=out_specs, check_vma=False)
```

```python
import functools
import math

import jax
import jax.numpy as jnp
from jax import lax
from jax.experimental import pallas as pl
from jax.experimental.pallas import tpu as pltpu
from jax.sharding import PartitionSpec as P

HEADS = 8
MESH = pl.DeviceIdType.MESH


def kernel(
    n,
    blocks,
    series_hbm,
    conv_hbm,
    qk_hbm,
    value_hbm,
    out_w_hbm,
    gain_hbm,
    out_ref,
    ext,
    conv_w,
    q_w,
    kv_w,
    out_w,
    gain,
    gathered,
    query_ref,
    key_ref,
    val_ref,
    load_sem,
    halo_send,
    halo_recv,
    peer_send,
    peer_recv,
    fwd_send,
    fwd_recv,
):
    steps, sens, width = out_ref.shape
    taps = conv_w.shape[0]
    lead = taps - 1
    pairs = n // 2
    head_dim = width // HEADS
    factor = math.log2(math.e) / math.sqrt(head_dim)
    me = lax.axis_index("sensor")
    here = lax.axis_index("tm")
    pair, core = me // 2, me % 2
    partner = pair * 2 + 1 - core

    loads = [
        pltpu.make_async_copy(series_hbm, ext.at[pl.ds(lead, steps)], load_sem.at[0]),
        pltpu.make_async_copy(conv_hbm, conv_w, load_sem.at[1]),
        pltpu.make_async_copy(qk_hbm.at[0], q_w, load_sem.at[2]),
        pltpu.make_async_copy(qk_hbm.at[1], kv_w.at[:, pl.ds(0, width)], load_sem.at[3]),
        pltpu.make_async_copy(value_hbm, kv_w.at[:, pl.ds(width, width)], load_sem.at[4]),
        pltpu.make_async_copy(out_w_hbm, out_w, load_sem.at[5]),
        pltpu.make_async_copy(gain_hbm, gain, load_sem.at[6]),
    ]
    for load in loads:
        load.start()

    def peer(j):
        return ((pair + j) % pairs) * 2 + core

    barrier = pltpu.get_barrier_semaphore()
    pl.semaphore_signal(barrier, inc=1, device_id={"sensor": partner}, device_id_type=MESH)
    for j in range(1, pairs):
        pl.semaphore_signal(barrier, inc=1, device_id={"sensor": peer(j)}, device_id_type=MESH)

    @pl.when(here > 0)
    def _():
        pl.semaphore_signal(barrier, inc=1, device_id={"tm": here - 1}, device_id_type=MESH)

    @pl.when(here < blocks - 1)
    def _():
        pl.semaphore_signal(barrier, inc=1, device_id={"tm": here + 1}, device_id_type=MESH)

    @pl.when(here == 0)
    def _():
        ext[pl.ds(0, lead)] = jnp.zeros((lead, sens, width), ext.dtype)

    val_ref[:, :, width:] = jnp.ones((steps, n * sens, width), val_ref.dtype)

    loads[0].wait()
    behind = (here + blocks - 1) // blocks
    ahead = (2 * blocks - 2 - here) // blocks
    pl.semaphore_wait(barrier, pairs + behind + ahead)

    def halo(i):
        return pltpu.make_async_remote_copy(
            src_ref=ext.at[steps + i],
            dst_ref=ext.at[i],
            send_sem=halo_send.at[i],
            recv_sem=halo_recv.at[i],
            device_id={"tm": here + 1},
            device_id_type=MESH,
        )

    @pl.when(here < blocks - 1)
    def _():
        for i in reversed(range(lead)):
            halo(i).start()

    def send(t, j):
        return pltpu.make_async_remote_copy(
            src_ref=gathered.at[t, 0, 0],
            dst_ref=gathered.at[t, j, 0],
            send_sem=peer_send.at[t, j],
            recv_sem=peer_recv.at[t, j],
            device_id={"sensor": peer(j)},
            device_id_type=MESH,
        )

    def forward(t, j):
        return pltpu.make_async_remote_copy(
            src_ref=gathered.at[t, j, 0],
            dst_ref=gathered.at[t, j, 1],
            send_sem=fwd_send.at[t, j],
            recv_sem=fwd_recv.at[t, j],
            device_id={"sensor": partner},
            device_id_type=MESH,
        )

    lanes = lax.broadcasted_iota(jnp.int32, (sens, width), 1)
    mine = [(lanes >= h * head_dim) & (lanes < (h + 1) * head_dim) for h in range(HEADS)]

    def prepare(t):
        if t < lead:

            @pl.when(here > 0)
            def _():
                halo(t).wait_recv()

        conv = jnp.dot(ext[lead + t], conv_w[0], preferred_element_type=jnp.float32)
        for tap in range(1, taps):
            conv = conv + jnp.dot(
                ext[lead + t - tap], conv_w[tap], preferred_element_type=jnp.float32
            )
        own = ext[lead + t].astype(jnp.float32)
        own = own + conv[:, :width] * jax.nn.sigmoid(conv[:, width:])
        gathered[t, 0, 0] = own.astype(gathered.dtype)
        for j in range(1, pairs):
            send(t, j).start()
        forward(t, 0).start()

    def queries(t):
        query = jnp.dot(gathered[t, 0, 0], q_w[...], preferred_element_type=jnp.float32)
        for h in range(HEADS):
            query_ref[t, h] = jnp.where(mine[h], query, 0.0).astype(jnp.bfloat16)

    def pass_on(t):
        for j in range(1, pairs):
            send(t, j).wait_recv()
            forward(t, j).start()

    def absorb(t, rows, start):
        count = rows.shape[0]
        place = pl.ds(start, count)
        both = jnp.dot(rows, kv_w[...], preferred_element_type=jnp.float32)
        key_ref[t, place] = both[:, :width].astype(jnp.bfloat16)
        val_ref[t, place, :width] = both[:, width:].astype(jnp.bfloat16)
        maxima = weighted = total = jnp.zeros((sens, width), jnp.float32)
        for h in range(HEADS):
            scores = lax.dot_general(
                query_ref[t, h],
                key_ref[t, place],
                (((1,), (1,)), ((), ())),
                preferred_element_type=jnp.float32,
            )
            top = jnp.max(scores, axis=-1, keepdims=True)
            probs = jnp.exp2((scores - top) * factor).astype(jnp.bfloat16)
            summed = jnp.dot(probs, val_ref[t, place], preferred_element_type=jnp.float32)
            maxima = jnp.where(mine[h], top, maxima)
            weighted = jnp.where(mine[h], summed[:, :width], weighted)
            total = jnp.where(mine[h], summed[:, width:], total)
        return maxima, weighted, total

    def merge(states):
        maxima = functools.reduce(jnp.maximum, [state[0] for state in states])
        weighted = total = 0.0
        for state in states:
            share = jnp.exp2((state[0] - maxima) * factor)
            weighted = weighted + state[1] * share
            total = total + state[2] * share
        return maxima, weighted, total

    states = [[] for _ in range(steps)]

    def half(t, side):
        if side:
            for j in range(pairs):
                forward(t, j).wait_recv()
        if pairs <= 4:
            rows = gathered[t, :, side].reshape(pairs * sens, width)
            states[t].append(absorb(t, rows, side * pairs * sens))
            return

        def one(j, state):
            return merge([state, absorb(t, gathered[t, j, side], 0)])

        start = absorb(t, gathered[t, 0, side], 0)
        states[t].append(lax.fori_loop(1, pairs, one, start))

    def finish(t):
        _, weighted, total = merge(states[t])
        attended = (weighted / total).astype(jnp.bfloat16)
        mixed = jnp.dot(attended, out_w[...], preferred_element_type=jnp.float32)
        mixed = mixed + gathered[t, 0, 0].astype(jnp.float32)
        mean = jnp.mean(mixed, axis=-1, keepdims=True)
        centred = mixed - mean
        var = jnp.mean(centred * centred, axis=-1, keepdims=True)
        normed = centred / jnp.sqrt(var + 1e-05) * gain[...]
        out_ref[t] = normed.astype(out_ref.dtype)

    last = steps - 1
    loads[1].wait()
    prepare(last)
    for load in loads[2:]:
        load.wait()
    queries(last)
    for t in reversed(range(last)):
        prepare(t)
        queries(t)
    pass_on(last)
    for t in reversed(range(steps)):
        half(t, 0)
        half(t, 1)
        if t > 0:
            pass_on(t - 1)
        finish(t)

    for t in range(steps):
        for j in range(1, pairs):
            send(t, j).wait_send()
        for j in range(pairs):
            forward(t, j).wait_send()

    @pl.when(here < blocks - 1)
    def _():
        for i in range(lead):
            halo(i).wait_send()


def solution(mesh):
    n, blocks = mesh.shape["sensor"], mesh.shape["tm"]

    def local(series, conv_weight, qk_weight, value_weight, out_weight, norm_gain):
        steps, sens, width = series.shape
        taps = conv_weight.shape[0]
        pairs = n // 2
        bf16 = jnp.bfloat16
        return pl.pallas_call(
            functools.partial(kernel, n, blocks),
            out_shape=jax.ShapeDtypeStruct(series.shape, bf16),
            in_specs=[pl.BlockSpec(memory_space=pl.ANY)] * 6,
            out_specs=pl.BlockSpec(memory_space=pltpu.VMEM),
            scratch_shapes=[
                pltpu.VMEM((taps - 1 + steps, sens, width), bf16),
                pltpu.VMEM(conv_weight.shape, bf16),
                pltpu.VMEM((width, width), bf16),
                pltpu.VMEM((width, 2 * width), bf16),
                pltpu.VMEM(out_weight.shape, bf16),
                pltpu.VMEM((1, width), jnp.float32),
                pltpu.VMEM((steps, pairs, 2, sens, width), bf16),
                pltpu.VMEM((steps, HEADS, sens, width), bf16),
                pltpu.VMEM((steps, n * sens, width), bf16),
                pltpu.VMEM((steps, n * sens, 2 * width), bf16),
                pltpu.SemaphoreType.DMA((7,)),
                pltpu.SemaphoreType.DMA((taps - 1,)),
                pltpu.SemaphoreType.DMA((taps - 1,)),
                pltpu.SemaphoreType.DMA((steps, pairs)),
                pltpu.SemaphoreType.DMA((steps, pairs)),
                pltpu.SemaphoreType.DMA((steps, pairs)),
                pltpu.SemaphoreType.DMA((steps, pairs)),
            ],
            compiler_params=pltpu.CompilerParams(collective_id=0, has_side_effects=True),
        )(
            series,
            conv_weight,
            qk_weight,
            value_weight,
            out_weight,
            norm_gain.reshape(1, width),
        )

    in_specs = (P("tm", "sensor", None), P(), P(), P(), P(), P())
    out_specs = P("tm", "sensor", None)
    return jax.shard_map(local, mesh=mesh, in_specs=in_specs, out_specs=out_specs, check_vma=False)
```
